32 devices in a mesh: pole: 4 (over z), row: 4 (over y, x), col: 2 (over core).
Axes of the slice: x: 2, y: 2, z: 4, core: 2. Of those that a mesh axis runs over, the one named last changes fastest.
Arguments:
- green_blocks: bfloat16 [16, 2, 192, 1536], P('pole', 'col', None, 'row'), parts along dimension 0, may hold values from -0.15625 to 0.15625
- lower_panel: bfloat16 [1536, 32, 128], P(('row', 'col'), 'pole'), parts along dimension 1, may hold values from -1.5 to 1.5
- pattern: int32 [12, 8], replicated, may hold values 0 or 1
- pivot_inverse: float32 [8, 512, 128], P(('row', 'col'), 'pole'), parts along dimension 1, may hold values from -6 to 6
Outputs:
- green_panel: bfloat16 [6144, 8, 128], P('pole', ('row', 'col')), parts along dimension 0
- green_diag: float32 [8, 512, 128], P(('row', 'col'), 'pole'), parts along dimension 1
The draws below stay inside these ranges and needn't reach their ends.
There are 4 independent parts, one for each index of `pole`. The reference program is written for one: setup_inputs(seed, part) draws one part's arguments, and reference() takes and returns one part's arrays. A program takes and returns all parts, laid end to end along the dimension named above; an argument that names none is the same for every part. Nothing has to cross between parts.
All inputs are finite; a program needn't handle non-finite values.
Results may differ from the reference program's by a relative error of at most 0.01.
Values may be sent and summed in bfloat16 or wider, within the bound.
A program may use at most 128 MiB of HBM per device.

```python
import jax
import jax.numpy as jnp
from jax import lax

BLK = 128
RDEV = 192
ORDER = 1536
NBLK = 12
NK = 8
N_ROW = 4
N_COL = 2


def place_ends(values, own_key, low, top_value):
    spot = [jax.random.randint(jax.random.fold_in(own_key, axis), (), 0, length) for axis, length in enumerate(values.shape)]
    main_axis = values.shape.index(max(values.shape))
    beside = spot[:main_axis] + [(spot[main_axis] + 1) % values.shape[main_axis]] + spot[main_axis + 1:]
    return values.at[tuple(spot)].set(low).at[tuple(beside)].set(top_value)


def with_spikes(array, own_key, source, target, blocks, factor):
    def block_of(dim):
        return (jnp.arange(array.shape[dim]) // (array.shape[dim] // blocks)).reshape((-1,) + (1,) * (array.ndim - 1 - dim))

    first = jax.random.permutation(own_key, blocks)[block_of(target)]
    far = (block_of(target) + blocks // 2) % blocks
    return jnp.where((block_of(source) == first) | (block_of(source) == far), factor * array, array)


def steps_of(own_key, shape, shards, least, top_value):
    level = 1.0
    for position, shards_of in shards:
        steps = jax.random.uniform(jax.random.fold_in(jax.random.fold_in(own_key, 6), position), (shards_of,), jnp.float32, least / len(shards), top_value / len(shards))
        level = level * jnp.repeat(jnp.exp(steps), shape[position] // shards_of).reshape((-1,) + (1,) * (len(shape) - 1 - position))
    return level


def scatter_about(key, shape, spread, reach, cuts=(), dtype=jnp.bfloat16):
    drawn = jax.random.normal(key, shape, jnp.float32) * spread
    if len(cuts) > 0:
        drawn = steps_of(key, shape, cuts, -0.22, 0.18) * drawn
    return jnp.clip(drawn, min=-reach, max=reach).astype(dtype)


def gaussian_with(rng, extent, spread, bound, cuts, heavy, kind=jnp.bfloat16):
    values = spread * jax.random.normal(rng, extent, jnp.float32)
    if cuts:
        values = values * steps_of(rng, extent, cuts, -0.22, 0.18)
    return jnp.clip(with_spikes(values, jax.random.fold_in(rng, 3), *heavy), -bound, bound).astype(kind)


def setup_inputs(seed: int = 0, part: int = 0) -> dict:
    seeds = jax.random.split(jax.random.key(seed), 5)
    own_keys = jax.random.split(jax.random.fold_in(seeds[4], part), 5)
    green_blocks = scatter_about(own_keys[0], (N_ROW, N_COL, RDEV, ORDER), ORDER ** -0.5, 0.15625, ((1, 2), (3, 4)))
    lower_panel = gaussian_with(own_keys[1], (ORDER, NK, BLK), 0.25, 1.5, ((0, 8),), (0, 1, 8, 2.0))
    pattern = place_ends((jax.random.randint(seeds[2], (NBLK, NK), 0, 2) < 1).astype(jnp.int32), jax.random.fold_in(seeds[2], 1), 0, 1)
    pivot_inverse = scatter_about(own_keys[3], (NK, BLK, BLK), 1.0, 6.0, ((0, 8),), jnp.float32)
    return dict(green_blocks=green_blocks, lower_panel=lower_panel, pattern=pattern, pivot_inverse=pivot_inverse)


def reference(green_blocks, lower_panel, pattern, pivot_inverse):
    matrix = green_blocks.reshape(ORDER, ORDER)
    row_mask = jnp.repeat(pattern, BLK, axis=0)
    masked = lower_panel * row_mask[:, :, None].astype(jnp.bfloat16)
    flat = masked.reshape(ORDER, NK * BLK)
    span = ORDER // N_ROW
    product = jnp.zeros((ORDER, NK * BLK), jnp.float32)
    for index in range(N_ROW):
        piece = jnp.dot(matrix[:, index * span:(index + 1) * span], flat[index * span:(index + 1) * span], preferred_element_type=jnp.float32)
        rounded = lax.optimization_barrier(piece.astype(jnp.bfloat16))
        product = product + rounded.astype(jnp.float32)
    resolved = product.reshape(ORDER, NK, BLK)
    green_panel = (-(resolved * row_mask[:, :, None].astype(jnp.float32))).astype(jnp.bfloat16)
    green_diag = pivot_inverse + jnp.einsum("rkb,rkc->kbc", masked.astype(jnp.float32), resolved, precision=lax.Precision.HIGHEST)
    return green_panel, green_diag
```

```python
import functools
import math

import jax
import jax.numpy as jnp
from jax import lax
from jax.experimental import pallas as pl
from jax.experimental.pallas import tpu as pltpu
from jax.sharding import PartitionSpec as P

MESH = pl.DeviceIdType.MESH
PAIR = 2
SPLIT = 2


def exchange(
    rows, cols, pattern_hbm, green_hbm, panel_hbm, pivot_hbm,
    out_ref, diag_ref,
    pattern_ref, green, green_x, panel_ref, wide, pivot_ref, slab, slab_x, column,
    own, to_own, ysum, to_y, far_out, far_in, to_x, xsum,
    load, green_send, green_recv, slab_send, slab_recv, panel_send, panel_recv, share_send, share_recv,
    near_send, near_recv, late_send, late_recv, own_send, own_recv, y_send, y_recv, far_send, far_recv, x_send, x_recv,
):
    r, c = lax.axis_index("row"), lax.axis_index("col")
    me = r * cols + c
    share, supernodes, width = panel_ref.shape
    row_x, row_y, row_far = r + 1 - 2 * (r % 2), (r + 2) % 4, 3 - r
    last = rows - 1
    size = share // SPLIT
    chunks = [(j, s * size) for j in range(last) for s in range(SPLIT)]

    def remote(src, dst, send, recv, row, col):
        return pltpu.make_async_remote_copy(
            src_ref=src, dst_ref=dst, send_sem=send, recv_sem=recv,
            device_id={"row": row, "col": col}, device_id_type=MESH,
        )

    started = []

    def start(copy):
        copy.start()
        started.append(copy)

    def arrived(place, send, recv):
        remote(place, place, send, recv, row_x, c).wait_recv()

    barrier = pltpu.get_barrier_semaphore()
    for row in (row_x, row_y):
        for k in range(cols):
            pl.semaphore_signal(barrier, 1, device_id={"row": row, "col": k}, device_id_type=MESH)
    for step in range(1, cols):
        pl.semaphore_signal(barrier, 1, device_id={"row": r, "col": (c + step) % cols}, device_id_type=MESH)
    loads = [
        pltpu.make_async_copy(panel_hbm, panel_ref, load.at[0]),
        pltpu.make_async_copy(pattern_hbm, pattern_ref, load.at[3]),
        pltpu.make_async_copy(green_hbm, green, load.at[1]),
        pltpu.make_async_copy(pivot_hbm, pivot_ref, load.at[2]),
    ]
    for copy in loads:
        copy.start()
    pl.semaphore_wait(barrier, 3 * cols - 1)

    def send_green(i):
        j, a = chunks[i]
        start(remote(
            green_hbm.at[j, pl.ds(a, size)], green_x.at[j, pl.ds(a, size)],
            green_send.at[i], green_recv.at[i], row_x, c,
        ))

    send_green(0)

    loads[0].wait()
    loads[1].wait()
    wide[...] = panel_ref[...].astype(jnp.float32).reshape(share * supernodes, width)
    piece = math.gcd(share, width)
    for k in range(supernodes):
        value = wide[pl.ds(k, share, stride=supernodes), :]
        parts = []
        for q in range(share // piece):
            flag = pattern_ref[k, (me * share + q * piece) // width].astype(jnp.float32)
            parts.append(value[q * piece:(q + 1) * piece] * flag)
        slab[c, k] = jnp.concatenate(parts, axis=0).astype(jnp.bfloat16)

    def group(row):
        return pl.ds(row * cols, cols)

    for g, row in ((1, row_far), (0, row_x)):
        start(remote(
            slab.at[c, group(row)], slab_x.at[c, g], panel_send.at[g], panel_recv.at[g], row_x, c,
        ))
    for k in range(cols):
        start(remote(
            slab.at[c, row_y * cols + k], column.at[me], near_send.at[k], near_recv.at[c], row_y, k,
        ))
    for step in range(1, cols):
        k = (c + step) % cols
        start(remote(slab.at[c], slab.at[c], slab_send.at[k], slab_recv.at[c], r, k))
    for i in range(1, len(chunks)):
        send_green(i)
    loads[2].wait()
    for step in range(1, cols):
        k = (c + step) % cols
        arrived(slab.at[k], slab_send.at[k], slab_recv.at[k])

    def pairs(body):
        if cols == PAIR:
            body(0)
        else:
            lax.fori_loop(0, cols // PAIR, lambda i, z: (body(i * PAIR), z)[1], 0)

    def stack(pick, k):
        return jnp.concatenate(
            [jnp.concatenate([pick(s, k + p) for s in range(cols)], axis=0) for p in range(PAIR)], axis=1
        )

    def alone(put, row):
        def body(k):
            rhs = stack(lambda s, q: slab[s, row * cols + q], k)
            value = jnp.dot(green[last], rhs, preferred_element_type=jnp.float32).astype(jnp.bfloat16)
            for p in range(PAIR):
                put(k + p, value[:, p * width:(p + 1) * width])

        pairs(body)

    def both(put, i, g, row):
        j, a = chunks[i]

        def body(k):
            rhs = jnp.concatenate(
                [stack(lambda s, q: slab[s, row * cols + q], k), stack(lambda s, q: slab_x[s, g, q], k)], axis=0
            )
            lhs = jnp.concatenate([green[j, a:a + size], green_x[j, a:a + size]], axis=1)
            value = jnp.dot(lhs, rhs, preferred_element_type=jnp.float32).astype(jnp.bfloat16)
            for p in range(PAIR):
                put(k + p, value[:, p * width:(p + 1) * width])

        pairs(body)

    def into(buffer, *at):
        def put(k, value):
            buffer[(k,) + at] = value
        return put

    alone(into(far_out), row_far)
    start(remote(far_out, far_in, far_send.at[0], far_recv.at[0], row_y, c))
    alone(into(to_y, last), row_y)
    count = len(chunks)
    for k in range(cols):
        start(remote(to_y.at[k, last], ysum.at[c, last], y_send.at[count, k], y_recv.at[count, c], row_y, k))
    alone(into(to_own, last), r)
    for step in range(1, cols):
        k = (c + step) % cols
        start(remote(to_own.at[k, last], own.at[c, last], own_send.at[count, k], own_recv.at[count, c], r, k))
    own[c, last] = to_own[c, last]
    alone(into(to_x), row_x)

    for g in (1, 0):
        arrived(slab_x.at[c, g], panel_send.at[g], panel_recv.at[g])
        for step in range(1, cols):
            k = (c + step) % cols
            start(remote(slab_x.at[c, g], slab_x.at[c, g], share_send.at[g, k], share_recv.at[g, c], r, k))
        if g == 1:
            for k in range(cols):
                start(remote(
                    slab_x.at[c, 1, k], column.at[row_x * cols + c], late_send.at[k], late_recv.at[c], row_y, k,
                ))

    def shared(g):
        for step in range(1, cols):
            k = (c + step) % cols
            arrived(slab_x.at[k, g], share_send.at[g, k], share_recv.at[g, k])

    def send_sum(i):
        j, a = chunks[i]
        arrived(green_x.at[j, pl.ds(a, size)], green_send.at[i], green_recv.at[i])
        both(into(to_y, j, slice(a, a + size)), i, 1, row_y)
        for k in range(cols):
            start(remote(
                to_y.at[k, j, pl.ds(a, size)], ysum.at[c, j, pl.ds(a, size)],
                y_send.at[i, k], y_recv.at[i, c], row_y, k,
            ))

    def keep_sum(i):
        j, a = chunks[i]
        both(into(to_own, j, slice(a, a + size)), i, 0, r)
        for step in range(1, cols):
            k = (c + step) % cols
            start(remote(
                to_own.at[k, j, pl.ds(a, size)], own.at[c, j, pl.ds(a, size)],
                own_send.at[i, k], own_recv.at[i, c], r, k,
            ))
        own[c, j, a:a + size] = to_own[c, j, a:a + size]

    def finish(i, j, a, n, late):
        for step in range(1, cols):
            k = (c + step) % cols
            arrived(own.at[k, j, pl.ds(a, n)], own_send.at[i, k], own_recv.at[i, k])
        for k in range(cols):
            arrived(ysum.at[k, j, pl.ds(a, n)], y_send.at[i, k], y_recv.at[i, k])
        cuts = sorted({a, a + n} | set(range(-(-a // piece) * piece, a + n, piece)))
        held = []
        for k in range(cols):
            begin = (j * cols + k) * share
            terms = [own[k, j, a:a + n], ysum[k, j, a:a + n]] + ([late[k, a:a + n]] if late is not None else [])
            held.append(jnp.concatenate(terms, axis=1))
            value = sum(term.astype(jnp.float32) for term in terms)
            for low, high in zip(cuts[:-1], cuts[1:]):
                flag = pattern_ref[me, (begin + low) // width].astype(jnp.float32)
                out_ref[begin + low:begin + high] = (-(value[low - a:high - a] * flag)).astype(jnp.bfloat16)
        lhs = jnp.concatenate([column[j * cols + k, a:a + n] for k in range(cols)], axis=0)
        grown = lax.dot_general(
            lhs, jnp.concatenate(held, axis=0), (((0,), (0,)), ((), ())), preferred_element_type=jnp.float32,
        )
        total = diag_ref[...]
        for t in range(grown.shape[1] // width):
            total = total + grown[:, t * width:(t + 1) * width]
        diag_ref[...] = total

    shared(1)
    send_sum(0)
    arrived(far_in, far_send.at[0], far_recv.at[0])
    to_x[...] = (to_x[...].astype(jnp.float32) + far_in[...].astype(jnp.float32)).astype(jnp.bfloat16)
    for k in range(cols):
        start(remote(to_x.at[k], xsum.at[c], x_send.at[k], x_recv.at[c], row_x, k))
    shared(0)
    keep_sum(0)
    send_sum(1)
    keep_sum(1)
    for s in range(cols):
        column[r * cols + s] = slab[s, me]
        column[row_x * cols + s] = slab_x[s, 0, c]
    loads[3].wait()
    diag_ref[...] = pivot_ref[...]
    for k in range(cols):
        place = column.at[row_y * cols + k]
        arrived(place, near_send.at[k], near_recv.at[k])
    for i in range(2, count):
        send_sum(i)
        keep_sum(i)
        if i == 2:
            for k in range(cols):
                place = column.at[row_far * cols + k]
                arrived(place, late_send.at[k], late_recv.at[k])
        if i >= 3:
            finish(i - 3, *chunks[i - 3], size, None)
    for i in range(count - 3, count - 1):
        finish(i, *chunks[i], size, None)
    for k in range(cols):
        arrived(xsum.at[k], x_send.at[k], x_recv.at[k])
    finish(count, last, 0, share, xsum)
    finish(count - 1, *chunks[count - 1], size, None)
    for copy in started:
        copy.wait_send()


def store(made, grown, out_ref, diag_ref, sems):
    copies = [pltpu.make_async_copy(made, out_ref, sems.at[0]), pltpu.make_async_copy(grown, diag_ref, sems.at[1])]
    for copy in copies:
        copy.start()
    for copy in copies:
        copy.wait()


def local(green_blocks, lower_panel, pattern, pivot_inverse):
    rows, cols = lax.axis_size("row"), lax.axis_size("col")
    share, supernodes, width = lower_panel.shape
    vmem = pl.BlockSpec(memory_space=pltpu.VMEM)
    hbm = pl.BlockSpec(memory_space=pltpu.HBM)
    bf16 = lambda *shape: pltpu.VMEM(shape, jnp.bfloat16)
    dma = lambda *shape: pltpu.SemaphoreType.DMA(shape)
    green = green_blocks.reshape(rows, share, -1)
    depth = green.shape[2]
    count = (rows - 1) * SPLIT
    buffers = [
        bf16(*green.shape),
        bf16(rows - 1, share, depth),
        bf16(*lower_panel.shape),
        pltpu.VMEM((share * supernodes, width), jnp.float32),
        pltpu.VMEM((width, width), jnp.float32),
        bf16(cols, supernodes, share, width),
        bf16(cols, 2, cols, share, width),
        bf16(rows * cols, share, width),
        bf16(cols, rows, share, width),
        bf16(cols, rows, share, width),
        bf16(cols, rows, share, width),
        bf16(cols, rows, share, width),
        bf16(cols, share, width),
        bf16(cols, share, width),
        bf16(cols, share, width),
        bf16(cols, share, width),
    ]
    held = sum(math.prod(b.shape) * jnp.dtype(b.dtype).itemsize for b in buffers)
    middle = pl.pallas_call(
        functools.partial(exchange, rows, cols),
        out_shape=(
            pltpu.VMEM((rows * cols * share, width), jnp.bfloat16),
            pltpu.VMEM((width, width), jnp.float32),
        ),
        in_specs=[hbm] * 4,
        out_specs=(vmem,) * 2,
        scratch_shapes=[pltpu.SMEM(pattern.shape[::-1], pattern.dtype)] + buffers + [
            dma(4), dma(count), dma(count), dma(cols), dma(cols), dma(2), dma(2), dma(2, cols), dma(2, cols),
            dma(cols), dma(cols), dma(cols), dma(cols), dma(count + 1, cols), dma(count + 1, cols),
            dma(count + 1, cols), dma(count + 1, cols), dma(1), dma(1), dma(cols), dma(cols),
        ],
        compiler_params=pltpu.CompilerParams(
            collective_id=0, has_side_effects=True, vmem_limit_bytes=held + held // 4 + 4 * 1024 * 1024,
        ),
    )(*(pltpu.with_memory_space_constraint(a, pltpu.HBM) for a in (pattern.T, green, lower_panel, pivot_inverse.reshape(width, width))))
    out, diag = pl.pallas_call(
        store,
        out_shape=(
            jax.ShapeDtypeStruct((rows * cols * share, width), jnp.bfloat16),
            jax.ShapeDtypeStruct((width, width), jnp.float32),
        ),
        in_specs=[vmem] * 2,
        out_specs=(hbm, hbm),
        scratch_shapes=[dma(2)],
        compiler_params=pltpu.CompilerParams(vmem_limit_bytes=16 * 1024 * 1024),
    )(*middle)
    return out.reshape(-1, 1, width), diag.reshape(1, width, width)


def solution(mesh):
    placed = (
        P("pole", "col", None, "row"),
        P(("row", "col"), "pole", None),
        P(),
        P(("row", "col"), "pole", None),
    )
    return jax.shard_map(
        local,
        mesh=mesh,
        in_specs=placed,
        out_specs=(P("pole", ("row", "col"), None), P(("row", "col"), "pole", None)),
        check_vma=False,
    )
```

```python
import functools
import math

import jax
import jax.numpy as jnp
from jax import lax
from jax.experimental import pallas as pl
from jax.experimental.pallas import tpu as pltpu
from jax.sharding import PartitionSpec as P

MESH = pl.DeviceIdType.MESH
PAIR = 2
STEPS = (7, 7, 6, 5, 4, 3)


def plan(total):
    unit = total // 3 * 2 // sum(STEPS) // 16 * 16
    ends = [0]
    for step in STEPS:
        ends.append(ends[-1] + step * unit)
    return list(zip(ends[:-1], ends[1:]))


def exchange(
    rows, cols, pattern_hbm, green_hbm, panel_hbm, pivot_hbm,
    out_ref, diag_ref,
    pattern_ref, green, green_x, panel_ref, wide, pivot_ref, slab, slab_x, column,
    own, to_own, ysum, to_y, far_out, far_in, to_x, xsum,
    load, green_recv, y_recv, own_recv, panel_recv, share_recv, one_recv, sent,
):
    r, c = lax.axis_index("row"), lax.axis_index("col")
    me = r * cols + c
    share, supernodes, width = panel_ref.shape
    row_x, row_y, row_far = r + 1 - 2 * (r % 2), (r + 2) % 4, 3 - r
    total = rows * share
    chunks = plan(total)
    count = len(chunks)
    split = chunks[-1][1]
    tail = slice(split, total)
    slab_recv, near_recv, late_recv, far_recv, x_recv = (one_recv.at[i] for i in range(5))
    (
        green_sent, panel_sent, slab_sent, share_sent, near_sent, late_sent, own_sent, y_sent, far_sent, x_sent
    ) = (sent.at[i] for i in range(10))

    def start(src, dst, send, recv, row, col):
        pltpu.make_async_remote_copy(
            src_ref=src, dst_ref=dst, send_sem=send, recv_sem=recv,
            device_id={"row": row, "col": col}, device_id_type=MESH,
        ).start()

    def arrived(place, recv):
        pltpu.make_async_copy(place, place, recv).wait()

    others = [(c + step) % cols for step in range(1, cols)]
    barrier = pltpu.get_barrier_semaphore()
    for row in (row_x, row_y):
        for k in range(cols):
            pl.semaphore_signal(barrier, 1, device_id={"row": row, "col": k}, device_id_type=MESH)
    for k in others:
        pl.semaphore_signal(barrier, 1, device_id={"row": r, "col": k}, device_id_type=MESH)
    loads = [
        pltpu.make_async_copy(panel_hbm, panel_ref, load.at[0]),
        pltpu.make_async_copy(pattern_hbm, pattern_ref, load.at[3]),
        pltpu.make_async_copy(green_hbm, green, load.at[1]),
        pltpu.make_async_copy(pivot_hbm, pivot_ref, load.at[2]),
    ]
    for copy in loads:
        copy.start()

    loads[0].wait()
    loads[1].wait()
    wide[...] = panel_ref[...].astype(jnp.float32).reshape(share * supernodes, width)
    piece = math.gcd(share, width)
    for k in range(supernodes):
        value = wide[pl.ds(k, share, stride=supernodes), :]
        parts = []
        for q in range(share // piece):
            flag = pattern_ref[k, (me * share + q * piece) // width].astype(jnp.float32)
            parts.append(value[q * piece:(q + 1) * piece] * flag)
        slab[c, k] = jnp.concatenate(parts, axis=0).astype(jnp.bfloat16)
    loads[2].wait()
    loads[3].wait()
    diag_ref[...] = pivot_ref[...]
    pl.semaphore_wait(barrier, 3 * cols - 1)

    def group(row):
        return pl.ds(row * cols, cols)

    for g, row in ((1, row_far), (0, row_x)):
        start(slab.at[c, group(row)], slab_x.at[c, g], panel_sent, panel_recv.at[g], row_x, c)
    for k in others:
        start(slab.at[c], slab.at[c], slab_sent, slab_recv, r, k)
    for k in range(cols):
        start(slab.at[c, row_y * cols + k], column.at[me], near_sent, near_recv, row_y, k)
    for i, (low, high) in enumerate(chunks):
        span = pl.ds(low, high - low)
        start(green.at[span], green_x.at[span], green_sent, green_recv.at[i], row_x, c)

    def pairs(body):
        if cols == PAIR:
            body(0)
        else:
            lax.fori_loop(0, cols // PAIR, lambda i, z: (body(i * PAIR), z)[1], 0)

    def stack(pick, k):
        return jnp.concatenate(
            [jnp.concatenate([pick(s, k + p) for s in range(cols)], axis=0) for p in range(PAIR)], axis=1
        )

    def product(buffer, at, lhs, rhs):
        def body(k):
            value = jnp.dot(lhs(), rhs(k), preferred_element_type=jnp.float32).astype(jnp.bfloat16)
            for p in range(PAIR):
                buffer[k + p, at] = value[:, p * width:(p + 1) * width]

        pairs(body)

    def alone(buffer, at, row):
        product(buffer, at, lambda: green[tail], lambda k: stack(lambda s, q: slab[s, row * cols + q], k))

    def joint(buffer, i, g, row):
        at = slice(*chunks[i])
        product(
            buffer, at,
            lambda: jnp.concatenate([green[at], green_x[at]], axis=1),
            lambda k: jnp.concatenate(
                [stack(lambda s, q: slab[s, row * cols + q], k), stack(lambda s, q: slab_x[s, g, q], k)], axis=0
            ),
        )

    rest = pl.ds(split, total - split)
    arrived(slab.at[pl.ds(0, cols - 1)], slab_recv)
    alone(far_out, slice(None), row_far)
    start(far_out, far_in, far_sent, far_recv, row_y, c)
    alone(to_y, tail, row_y)
    for k in range(cols):
        start(to_y.at[k, rest], ysum.at[c, rest], y_sent, y_recv.at[count], row_y, k)
    alone(to_own, tail, r)
    for k in others:
        start(to_own.at[k, rest], own.at[c, rest], own_sent, own_recv.at[count], r, k)
    own[c, tail] = to_own[c, tail]
    alone(to_x, slice(None), row_x)

    def pass_on(g):
        arrived(slab_x.at[c, g], panel_recv.at[g])
        for k in others:
            start(slab_x.at[c, g], slab_x.at[c, g], share_sent, share_recv.at[g], r, k)

    def shared(g):
        arrived(slab_x.at[pl.ds(0, cols - 1), g], share_recv.at[g])

    pass_on(1)
    for k in range(cols):
        start(slab_x.at[c, 1, k], column.at[row_x * cols + c], late_sent, late_recv, row_y, k)
    pass_on(0)
    arrived(far_in, far_recv)
    to_x[...] = (to_x[...].astype(jnp.float32) + far_in[...].astype(jnp.float32)).astype(jnp.bfloat16)
    for k in range(cols):
        start(to_x.at[k], xsum.at[c], x_sent, x_recv, row_x, k)

    def send_sum(i):
        low, high = chunks[i]
        span = pl.ds(low, high - low)
        arrived(green_x.at[span], green_recv.at[i])
        joint(to_y, i, 1, row_y)
        for k in range(cols):
            start(to_y.at[k, span], ysum.at[c, span], y_sent, y_recv.at[i], row_y, k)

    def keep_sum(i):
        low, high = chunks[i]
        span = pl.ds(low, high - low)
        joint(to_own, i, 0, r)
        for k in others:
            start(to_own.at[k, span], own.at[c, span], own_sent, own_recv.at[i], r, k)
        own[c, low:high] = to_own[c, low:high]

    def finish(i, low, high, late):
        span = pl.ds(low, high - low)
        arrived(own.at[pl.ds(0, cols - 1), span], own_recv.at[i])
        arrived(ysum.at[:, span], y_recv.at[i])
        lhs, rhs = [], []
        for k in range(cols):
            terms = [own[k, low:high], ysum[k, low:high]] + ([late[k]] if late is not None else [])
            rhs.append(jnp.concatenate(terms, axis=1))
            value = sum(term.astype(jnp.float32) for term in terms)
            cuts = sorted({low, high} | set(range(-(-low // piece) * piece, high, piece)))
            for first, end in zip(cuts[:-1], cuts[1:]):
                begin = (first // share * cols + k) * share + first % share
                flag = pattern_ref[me, begin // width].astype(jnp.float32)
                out_ref[begin:begin + end - first] = (-(value[first - low:end - low] * flag)).astype(jnp.bfloat16)
            cuts = sorted({low, high} | set(range(-(-low // share) * share, high, share)))
            for first, end in zip(cuts[:-1], cuts[1:]):
                a = first % share
                lhs.append(column[first // share * cols + k, a:a + end - first])
        grown = lax.dot_general(
            jnp.concatenate(lhs, axis=0), jnp.concatenate(rhs, axis=0),
            (((0,), (0,)), ((), ())), preferred_element_type=jnp.float32,
        )
        value = diag_ref[...]
        for t in range(grown.shape[1] // width):
            value = value + grown[:, t * width:(t + 1) * width]
        diag_ref[...] = value

    shared(1)
    send_sum(0)
    shared(0)
    keep_sum(0)
    for s in range(cols):
        column[r * cols + s] = slab[s, me]
        column[row_x * cols + s] = slab_x[s, 0, c]
    send_sum(1)
    keep_sum(1)
    send_sum(2)
    keep_sum(2)
    arrived(column.at[group(row_y)], near_recv)
    arrived(column.at[group(row_far)], late_recv)
    for i in range(3, count):
        send_sum(i)
        keep_sum(i)
        finish(i - 3, *chunks[i - 3], None)
    for i in range(count - 3, count - 1):
        finish(i, *chunks[i], None)
    arrived(xsum, x_recv)
    finish(count, split, total, xsum)
    finish(count - 1, *chunks[count - 1], None)
    for place, sem in (
        (green_x, green_sent), (slab_x.at[0], panel_sent), (slab.at[pl.ds(0, cols - 1)], slab_sent),
        (slab_x.at[pl.ds(0, cols - 1)], share_sent), (column.at[pl.ds(0, cols)], near_sent),
        (column.at[pl.ds(0, cols)], late_sent), (own.at[pl.ds(0, cols - 1)], own_sent), (ysum, y_sent),
        (far_out, far_sent), (to_x, x_sent),
    ):
        arrived(place, sem)


def store(made, grown, out_ref, diag_ref, sems):
    copies = [pltpu.make_async_copy(made, out_ref, sems.at[0]), pltpu.make_async_copy(grown, diag_ref, sems.at[1])]
    for copy in copies:
        copy.start()
    for copy in copies:
        copy.wait()


def local(green_blocks, lower_panel, pattern, pivot_inverse):
    rows, cols = lax.axis_size("row"), lax.axis_size("col")
    share, supernodes, width = lower_panel.shape
    vmem = pl.BlockSpec(memory_space=pltpu.VMEM)
    hbm = pl.BlockSpec(memory_space=pltpu.HBM)
    bf16 = lambda *shape: pltpu.VMEM(shape, jnp.bfloat16)
    dma = lambda *shape: pltpu.SemaphoreType.DMA(shape)
    total = rows * share
    green = green_blocks.reshape(total, -1)
    depth = green.shape[1]
    chunks = plan(total)
    count, split = len(chunks), chunks[-1][1]
    buffers = [
        bf16(total, depth),
        bf16(split, depth),
        bf16(*lower_panel.shape),
        pltpu.VMEM((share * supernodes, width), jnp.float32),
        pltpu.VMEM((width, width), jnp.float32),
        bf16(cols, supernodes, share, width),
        bf16(cols, 2, cols, share, width),
        bf16(rows * cols, share, width),
        bf16(cols, total, width),
        bf16(cols, total, width),
        bf16(cols, total, width),
        bf16(cols, total, width),
        bf16(cols, total - split, width),
        bf16(cols, total - split, width),
        bf16(cols, total - split, width),
        bf16(cols, total - split, width),
    ]
    held = sum(math.prod(b.shape) * jnp.dtype(b.dtype).itemsize for b in buffers)
    middle = pl.pallas_call(
        functools.partial(exchange, rows, cols),
        out_shape=(
            pltpu.VMEM((cols * total, width), jnp.bfloat16),
            pltpu.VMEM((width, width), jnp.float32),
        ),
        in_specs=[hbm] * 4,
        out_specs=(vmem,) * 2,
        scratch_shapes=[pltpu.SMEM(pattern.shape[::-1], pattern.dtype)] + buffers + [
            dma(4), dma(count), dma(count + 1), dma(count + 1), dma(2), dma(2), dma(5), dma(10),
        ],
        compiler_params=pltpu.CompilerParams(
            collective_id=0, has_side_effects=True, vmem_limit_bytes=held + held // 4 + 4 * 1024 * 1024,
        ),
    )(*(pltpu.with_memory_space_constraint(a, pltpu.HBM) for a in (pattern.T, green, lower_panel, pivot_inverse.reshape(width, width))))
    out, diag = pl.pallas_call(
        store,
        out_shape=(
            jax.ShapeDtypeStruct((cols * total, width), jnp.bfloat16),
            jax.ShapeDtypeStruct((width, width), jnp.float32),
        ),
        in_specs=[vmem] * 2,
        out_specs=(hbm, hbm),
        scratch_shapes=[dma(2)],
        compiler_params=pltpu.CompilerParams(vmem_limit_bytes=16 * 1024 * 1024),
    )(*middle)
    return out.reshape(-1, 1, width), diag.reshape(1, width, width)


def solution(mesh):
    placed = (
        P("pole", "col", None, "row"),
        P(("row", "col"), "pole", None),
        P(),
        P(("row", "col"), "pole", None),
    )
    return jax.shard_map(
        local,
        mesh=mesh,
        in_specs=placed,
        out_specs=(P("pole", ("row", "col"), None), P(("row", "col"), "pole", None)),
        check_vma=False,
    )
```

```python
import functools
import math

import jax
import jax.numpy as jnp
from jax import lax
from jax.experimental import pallas as pl
from jax.experimental.pallas import tpu as pltpu
from jax.sharding import PartitionSpec as P

MESH = pl.DeviceIdType.MESH
PAIR = 2
LAG = 2
STEPS = (10, 9, 8, 3)


def plan(total):
    unit = total // 48
    ends = [0]
    for step in STEPS:
        ends.append(ends[-1] + step * unit)
    return list(zip(ends[:-1], ends[1:]))


def exchange(
    rows, cols, pattern_hbm, green_hbm, panel_hbm, pivot_hbm,
    out_ref, diag_ref,
    pattern_ref, green, green_x, panel_ref, wide, pivot_ref, slab, slab_x, column,
    own, to_own, ysum, to_y, far_out, far_in, to_x, xsum,
    load, green_recv, y_recv, own_recv, panel_recv, share_recv, one_recv, sent,
):
    r, c = lax.axis_index("row"), lax.axis_index("col")
    me = r * cols + c
    share, supernodes, width = panel_ref.shape
    row_x, row_y, row_far = r + 1 - 2 * (r % 2), (r + 2) % 4, 3 - r
    total = rows * share
    chunks = plan(total)
    count = len(chunks)
    split = chunks[-1][1]
    tail = slice(split, total)
    slab_recv, near_recv, late_recv, far_recv, x_recv = (one_recv.at[i] for i in range(5))
    (
        green_sent, panel_sent, slab_sent, share_sent, near_sent, late_sent, own_sent, y_sent, far_sent, x_sent
    ) = (sent.at[i] for i in range(10))

    def start(src, dst, send, recv, row, col):
        pltpu.make_async_remote_copy(
            src_ref=src, dst_ref=dst, send_sem=send, recv_sem=recv,
            device_id={"row": row, "col": col}, device_id_type=MESH,
        ).start()

    def arrived(place, recv):
        pltpu.make_async_copy(place, place, recv).wait()

    others = [(c + step) % cols for step in range(1, cols)]
    barrier = pltpu.get_barrier_semaphore()
    for row in (row_x, row_y):
        for k in range(cols):
            pl.semaphore_signal(barrier, 1, device_id={"row": row, "col": k}, device_id_type=MESH)
    for k in others:
        pl.semaphore_signal(barrier, 1, device_id={"row": r, "col": k}, device_id_type=MESH)
    loads = [
        pltpu.make_async_copy(panel_hbm, panel_ref, load.at[0]),
        pltpu.make_async_copy(pattern_hbm, pattern_ref, load.at[3]),
        pltpu.make_async_copy(green_hbm, green, load.at[1]),
        pltpu.make_async_copy(pivot_hbm, pivot_ref, load.at[2]),
    ]
    for copy in loads:
        copy.start()

    loads[0].wait()
    loads[1].wait()
    wide[...] = panel_ref[...].astype(jnp.float32).reshape(share * supernodes, width)
    piece = math.gcd(share, width)
    for k in range(supernodes):
        value = wide[pl.ds(k, share, stride=supernodes), :]
        parts = []
        for q in range(share // piece):
            flag = pattern_ref[k, (me * share + q * piece) // width].astype(jnp.float32)
            parts.append(value[q * piece:(q + 1) * piece] * flag)
        slab[c, k] = jnp.concatenate(parts, axis=0).astype(jnp.bfloat16)
    loads[2].wait()
    loads[3].wait()
    diag_ref[...] = pivot_ref[...]
    pl.semaphore_wait(barrier, 3 * cols - 1)

    def group(row):
        return pl.ds(row * cols, cols)

    for g, row in ((1, row_far), (0, row_x)):
        start(slab.at[c, group(row)], slab_x.at[c, g], panel_sent, panel_recv.at[g], row_x, c)
    for k in others:
        start(slab.at[c], slab.at[c], slab_sent, slab_recv, r, k)
    for k in range(cols):
        start(slab.at[c, row_y * cols + k], column.at[me], near_sent, near_recv, row_y, k)
    for i, (low, high) in enumerate(chunks):
        span = pl.ds(low, high - low)
        start(green.at[span], green_x.at[span], green_sent, green_recv.at[i], row_x, c)

    def pairs(body):
        if cols == PAIR:
            body(0)
        else:
            lax.fori_loop(0, cols // PAIR, lambda i, z: (body(i * PAIR), z)[1], 0)

    def stack(pick, k):
        return jnp.concatenate(
            [jnp.concatenate([pick(s, k + p) for s in range(cols)], axis=0) for p in range(PAIR)], axis=1
        )

    def product(buffer, at, lhs, rhs):
        def body(k):
            value = jnp.dot(lhs(), rhs(k), preferred_element_type=jnp.float32).astype(jnp.bfloat16)
            for p in range(PAIR):
                buffer[k + p, at] = value[:, p * width:(p + 1) * width]

        pairs(body)

    def alone(buffer, at, row):
        product(buffer, at, lambda: green[tail], lambda k: stack(lambda s, q: slab[s, row * cols + q], k))

    def joint(buffer, i, g, row):
        at = slice(*chunks[i])
        product(
            buffer, at,
            lambda: jnp.concatenate([green[at], green_x[at]], axis=1),
            lambda k: jnp.concatenate(
                [stack(lambda s, q: slab[s, row * cols + q], k), stack(lambda s, q: slab_x[s, g, q], k)], axis=0
            ),
        )

    rest = pl.ds(split, total - split)
    arrived(slab.at[pl.ds(0, cols - 1)], slab_recv)
    alone(far_out, slice(None), row_far)
    start(far_out, far_in, far_sent, far_recv, row_y, c)
    alone(to_y, tail, row_y)
    for k in range(cols):
        start(to_y.at[k, rest], ysum.at[c, rest], y_sent, y_recv.at[count], row_y, k)
    alone(to_own, tail, r)
    for k in others:
        start(to_own.at[k, rest], own.at[c, rest], own_sent, own_recv.at[count], r, k)
    own[c, tail] = to_own[c, tail]
    alone(to_x, slice(None), row_x)

    def pass_on(g):
        arrived(slab_x.at[c, g], panel_recv.at[g])
        for k in others:
            start(slab_x.at[c, g], slab_x.at[c, g], share_sent, share_recv.at[g], r, k)

    def shared(g):
        arrived(slab_x.at[pl.ds(0, cols - 1), g], share_recv.at[g])

    pass_on(1)
    for k in range(cols):
        start(slab_x.at[c, 1, k], column.at[row_x * cols + c], late_sent, late_recv, row_y, k)
    pass_on(0)
    arrived(far_in, far_recv)
    to_x[...] = (to_x[...].astype(jnp.float32) + far_in[...].astype(jnp.float32)).astype(jnp.bfloat16)
    for k in range(cols):
        start(to_x.at[k], xsum.at[c], x_sent, x_recv, row_x, k)

    def send_sum(i):
        low, high = chunks[i]
        span = pl.ds(low, high - low)
        arrived(green_x.at[span], green_recv.at[i])
        joint(to_y, i, 1, row_y)
        for k in range(cols):
            start(to_y.at[k, span], ysum.at[c, span], y_sent, y_recv.at[i], row_y, k)

    def keep_sum(i):
        low, high = chunks[i]
        span = pl.ds(low, high - low)
        joint(to_own, i, 0, r)
        for k in others:
            start(to_own.at[k, span], own.at[c, span], own_sent, own_recv.at[i], r, k)
        own[c, low:high] = to_own[c, low:high]

    def finish(i, low, high, late):
        span = pl.ds(low, high - low)
        arrived(own.at[pl.ds(0, cols - 1), span], own_recv.at[i])
        arrived(ysum.at[:, span], y_recv.at[i])
        lhs, rhs = [], []
        for k in range(cols):
            terms = [own[k, low:high], ysum[k, low:high]] + ([late[k]] if late is not None else [])
            rhs.append(jnp.concatenate(terms, axis=1))
            value = sum(term.astype(jnp.float32) for term in terms)
            cuts = sorted({low, high} | set(range(-(-low // piece) * piece, high, piece)))
            for first, end in zip(cuts[:-1], cuts[1:]):
                begin = (first // share * cols + k) * share + first % share
                flag = pattern_ref[me, begin // width].astype(jnp.float32)
                out_ref[begin:begin + end - first] = (-(value[first - low:end - low] * flag)).astype(jnp.bfloat16)
            cuts = sorted({low, high} | set(range(-(-low // share) * share, high, share)))
            for first, end in zip(cuts[:-1], cuts[1:]):
                a = first % share
                lhs.append(column[first // share * cols + k, a:a + end - first])
        grown = lax.dot_general(
            jnp.concatenate(lhs, axis=0), jnp.concatenate(rhs, axis=0),
            (((0,), (0,)), ((), ())), preferred_element_type=jnp.float32,
        )
        value = diag_ref[...]
        for t in range(grown.shape[1] // width):
            value = value + grown[:, t * width:(t + 1) * width]
        diag_ref[...] = value

    def columns():
        arrived(column.at[group(row_y)], near_recv)
        arrived(column.at[group(row_far)], late_recv)

    shared(1)
    send_sum(0)
    shared(0)
    keep_sum(0)
    for s in range(cols):
        column[r * cols + s] = slab[s, me]
        column[row_x * cols + s] = slab_x[s, 0, c]
    for i in range(1, count):
        send_sum(i)
        keep_sum(i)
        if i >= LAG:
            if i == LAG:
                columns()
            finish(i - LAG, *chunks[i - LAG], None)
    if count <= LAG:
        columns()
    for i in range(max(count - LAG, 0), count - 1):
        finish(i, *chunks[i], None)
    arrived(xsum, x_recv)
    finish(count, split, total, xsum)
    finish(count - 1, *chunks[count - 1], None)
    for place, sem in (
        (green_x, green_sent), (slab_x.at[0], panel_sent), (slab.at[pl.ds(0, cols - 1)], slab_sent),
        (slab_x.at[pl.ds(0, cols - 1)], share_sent), (column.at[pl.ds(0, cols)], near_sent),
        (column.at[pl.ds(0, cols)], late_sent), (own.at[pl.ds(0, cols - 1)], own_sent), (ysum, y_sent),
        (far_out, far_sent), (to_x, x_sent),
    ):
        arrived(place, sem)


def store(made, grown, out_ref, diag_ref, sems):
    copies = [pltpu.make_async_copy(made, out_ref, sems.at[0]), pltpu.make_async_copy(grown, diag_ref, sems.at[1])]
    for copy in copies:
        copy.start()
    for copy in copies:
        copy.wait()


def local(green_blocks, lower_panel, pattern, pivot_inverse):
    rows, cols = lax.axis_size("row"), lax.axis_size("col")
    share, supernodes, width = lower_panel.shape
    vmem = pl.BlockSpec(memory_space=pltpu.VMEM)
    hbm = pl.BlockSpec(memory_space=pltpu.HBM)
    bf16 = lambda *shape: pltpu.VMEM(shape, jnp.bfloat16)
    dma = lambda *shape: pltpu.SemaphoreType.DMA(shape)
    total = rows * share
    green = green_blocks.reshape(total, -1)
    depth = green.shape[1]
    chunks = plan(total)
    count, split = len(chunks), chunks[-1][1]
    buffers = [
        bf16(total, depth),
        bf16(split, depth),
        bf16(*lower_panel.shape),
        pltpu.VMEM((share * supernodes, width), jnp.float32),
        pltpu.VMEM((width, width), jnp.float32),
        bf16(cols, supernodes, share, width),
        bf16(cols, 2, cols, share, width),
        bf16(rows * cols, share, width),
        bf16(cols, total, width),
        bf16(cols, total, width),
        bf16(cols, total, width),
        bf16(cols, total, width),
        bf16(cols, total - split, width),
        bf16(cols, total - split, width),
        bf16(cols, total - split, width),
        bf16(cols, total - split, width),
    ]
    held = sum(math.prod(b.shape) * jnp.dtype(b.dtype).itemsize for b in buffers)
    middle = pl.pallas_call(
        functools.partial(exchange, rows, cols),
        out_shape=(
            pltpu.VMEM((cols * total, width), jnp.bfloat16),
            pltpu.VMEM((width, width), jnp.float32),
        ),
        in_specs=[hbm] * 4,
        out_specs=(vmem,) * 2,
        scratch_shapes=[pltpu.SMEM(pattern.shape[::-1], pattern.dtype)] + buffers + [
            dma(4), dma(count), dma(count + 1), dma(count + 1), dma(2), dma(2), dma(5), dma(10),
        ],
        compiler_params=pltpu.CompilerParams(
            collective_id=0, has_side_effects=True, vmem_limit_bytes=held + held // 4 + 4 * 1024 * 1024,
        ),
    )(*(pltpu.with_memory_space_constraint(a, pltpu.HBM) for a in (pattern.T, green, lower_panel, pivot_inverse.reshape(width, width))))
    out, diag = pl.pallas_call(
        store,
        out_shape=(
            jax.ShapeDtypeStruct((cols * total, width), jnp.bfloat16),
            jax.ShapeDtypeStruct((width, width), jnp.float32),
        ),
        in_specs=[vmem] * 2,
        out_specs=(hbm, hbm),
        scratch_shapes=[dma(2)],
        compiler_params=pltpu.CompilerParams(vmem_limit_bytes=16 * 1024 * 1024),
    )(*middle)
    return out.reshape(-1, 1, width), diag.reshape(1, width, width)


def solution(mesh):
    placed = (
        P("pole", "col", None, "row"),
        P(("row", "col"), "pole", None),
        P(),
        P(("row", "col"), "pole", None),
    )
    return jax.shard_map(
        local,
        mesh=mesh,
        in_specs=placed,
        out_specs=(P("pole", ("row", "col"), None), P(("row", "col"), "pole", None)),
        check_vma=False,
    )
```

```python
import functools
import math

import jax
import jax.numpy as jnp
from jax import lax
from jax.experimental import pallas as pl
from jax.experimental.pallas import tpu as pltpu
from jax.sharding import PartitionSpec as P

MESH = pl.DeviceIdType.MESH
PAIR = 2
LAG = 2
STEPS = (10, 10, 7, 3)


def plan(total):
    unit = total // 48
    ends = [0]
    for step in STEPS:
        ends.append(ends[-1] + step * unit)
    return list(zip(ends[:-1], ends[1:]))


def exchange(
    rows, cols, pattern_hbm, green_hbm, panel_hbm, pivot_hbm,
    out_ref, diag_ref,
    pattern_ref, green, green_x, panel_ref, wide, pivot_ref, slab, slab_x, column,
    own, to_own, ysum, to_y, far_out, far_in, to_x, xsum,
    load, green_recv, y_recv, own_recv, panel_recv, share_recv, one_recv, sent,
):
    r, c = lax.axis_index("row"), lax.axis_index("col")
    me = r * cols + c
    share, supernodes, width = panel_ref.shape
    row_x, row_y, row_far = r + 1 - 2 * (r % 2), (r + 2) % 4, 3 - r
    total = rows * share
    chunks = plan(total)
    count = len(chunks)
    split = chunks[-1][1]
    tail = slice(split, total)
    slab_recv, near_recv, late_recv, far_recv, x_recv = (one_recv.at[i] for i in range(5))
    (
        green_sent, panel_sent, slab_sent, share_sent, near_sent, late_sent, own_sent, y_sent, far_sent, x_sent
    ) = (sent.at[i] for i in range(10))

    def start(src, dst, send, recv, row, col):
        pltpu.make_async_remote_copy(
            src_ref=src, dst_ref=dst, send_sem=send, recv_sem=recv,
            device_id={"row": row, "col": col}, device_id_type=MESH,
        ).start()

    def arrived(place, recv):
        pltpu.make_async_copy(place, place, recv).wait()

    others = [(c + step) % cols for step in range(1, cols)]
    barrier = pltpu.get_barrier_semaphore()
    for row in (row_x, row_y):
        for k in range(cols):
            pl.semaphore_signal(barrier, 1, device_id={"row": row, "col": k}, device_id_type=MESH)
    for k in others:
        pl.semaphore_signal(barrier, 1, device_id={"row": r, "col": k}, device_id_type=MESH)
    loads = [
        pltpu.make_async_copy(panel_hbm, panel_ref, load.at[0]),
        pltpu.make_async_copy(pattern_hbm, pattern_ref, load.at[3]),
        pltpu.make_async_copy(green_hbm, green, load.at[1]),
        pltpu.make_async_copy(pivot_hbm, pivot_ref, load.at[2]),
    ]
    for copy in loads:
        copy.start()

    loads[0].wait()
    loads[1].wait()
    wide[...] = panel_ref[...].astype(jnp.float32).reshape(share * supernodes, width)
    piece = math.gcd(share, width)
    for k in range(supernodes):
        value = wide[pl.ds(k, share, stride=supernodes), :]
        parts = []
        for q in range(share // piece):
            flag = pattern_ref[k, (me * share + q * piece) // width].astype(jnp.float32)
            parts.append(value[q * piece:(q + 1) * piece] * flag)
        slab[c, k] = jnp.concatenate(parts, axis=0).astype(jnp.bfloat16)
    loads[2].wait()
    loads[3].wait()
    diag_ref[...] = pivot_ref[...]
    pl.semaphore_wait(barrier, 3 * cols - 1)

    def group(row):
        return pl.ds(row * cols, cols)

    for g, row in ((1, row_far), (0, row_x)):
        start(slab.at[c, group(row)], slab_x.at[c, g], panel_sent, panel_recv.at[g], row_x, c)
    for k in others:
        start(slab.at[c], slab.at[c], slab_sent, slab_recv, r, k)
    for k in range(cols):
        start(slab.at[c, row_y * cols + k], column.at[me], near_sent, near_recv, row_y, k)
    for i, (low, high) in enumerate(chunks):
        span = pl.ds(low, high - low)
        start(green.at[span], green_x.at[span], green_sent, green_recv.at[i], row_x, c)

    def pairs(body):
        if cols == PAIR:
            body(0)
        else:
            lax.fori_loop(0, cols // PAIR, lambda i, z: (body(i * PAIR), z)[1], 0)

    def stack(pick, k):
        return jnp.concatenate(
            [jnp.concatenate([pick(s, k + p) for s in range(cols)], axis=0) for p in range(PAIR)], axis=1
        )

    def product(buffer, at, lhs, rhs):
        def body(k):
            value = jnp.dot(lhs(), rhs(k), preferred_element_type=jnp.float32).astype(jnp.bfloat16)
            for p in range(PAIR):
                buffer[k + p, at] = value[:, p * width:(p + 1) * width]

        pairs(body)

    def alone(buffer, at, row):
        product(buffer, at, lambda: green[tail], lambda k: stack(lambda s, q: slab[s, row * cols + q], k))

    def joint(buffer, i, g, row):
        at = slice(*chunks[i])
        product(
            buffer, at,
            lambda: jnp.concatenate([green[at], green_x[at]], axis=1),
            lambda k: jnp.concatenate(
                [stack(lambda s, q: slab[s, row * cols + q], k), stack(lambda s, q: slab_x[s, g, q], k)], axis=0
            ),
        )

    rest = pl.ds(split, total - split)
    arrived(slab.at[pl.ds(0, cols - 1)], slab_recv)
    alone(far_out, slice(None), row_far)
    start(far_out, far_in, far_sent, far_recv, row_y, c)
    alone(to_y, tail, row_y)
    for k in range(cols):
        start(to_y.at[k, rest], ysum.at[c, rest], y_sent, y_recv.at[count], row_y, k)
    alone(to_own, tail, r)
    for k in others:
        start(to_own.at[k, rest], own.at[c, rest], own_sent, own_recv.at[count], r, k)
    own[c, tail] = to_own[c, tail]
    alone(to_x, slice(None), row_x)

    def pass_on(g):
        arrived(slab_x.at[c, g], panel_recv.at[g])
        for k in others:
            start(slab_x.at[c, g], slab_x.at[c, g], share_sent, share_recv.at[g], r, k)

    def shared(g):
        arrived(slab_x.at[pl.ds(0, cols - 1), g], share_recv.at[g])

    pass_on(1)
    for k in range(cols):
        start(slab_x.at[c, 1, k], column.at[row_x * cols + c], late_sent, late_recv, row_y, k)
    pass_on(0)
    arrived(far_in, far_recv)
    to_x[...] = (to_x[...].astype(jnp.float32) + far_in[...].astype(jnp.float32)).astype(jnp.bfloat16)
    for k in range(cols):
        start(to_x.at[k], xsum.at[c], x_sent, x_recv, row_x, k)

    def send_sum(i):
        low, high = chunks[i]
        span = pl.ds(low, high - low)
        arrived(green_x.at[span], green_recv.at[i])
        joint(to_y, i, 1, row_y)
        for k in range(cols):
            start(to_y.at[k, span], ysum.at[c, span], y_sent, y_recv.at[i], row_y, k)

    def keep_sum(i):
        low, high = chunks[i]
        span = pl.ds(low, high - low)
        joint(to_own, i, 0, r)
        for k in others:
            start(to_own.at[k, span], own.at[c, span], own_sent, own_recv.at[i], r, k)
        own[c, low:high] = to_own[c, low:high]

    def finish(i, low, high, late):
        span = pl.ds(low, high - low)
        arrived(own.at[pl.ds(0, cols - 1), span], own_recv.at[i])
        arrived(ysum.at[:, span], y_recv.at[i])
        lhs, rhs = [], []
        for k in range(cols):
            terms = [own[k, low:high], ysum[k, low:high]] + ([late[k]] if late is not None else [])
            rhs.append(jnp.concatenate(terms, axis=1))
            value = sum(term.astype(jnp.float32) for term in terms)
            cuts = sorted({low, high} | set(range(-(-low // piece) * piece, high, piece)))
            for first, end in zip(cuts[:-1], cuts[1:]):
                begin = (first // share * cols + k) * share + first % share
                flag = pattern_ref[me, begin // width].astype(jnp.float32)
                out_ref[begin:begin + end - first] = (-(value[first - low:end - low] * flag)).astype(jnp.bfloat16)
            cuts = sorted({low, high} | set(range(-(-low // share) * share, high, share)))
            for first, end in zip(cuts[:-1], cuts[1:]):
                a = first % share
                lhs.append(column[first // share * cols + k, a:a + end - first])
        grown = lax.dot_general(
            jnp.concatenate(lhs, axis=0), jnp.concatenate(rhs, axis=0),
            (((0,), (0,)), ((), ())), preferred_element_type=jnp.float32,
        )
        value = diag_ref[...]
        for t in range(grown.shape[1] // width):
            value = value + grown[:, t * width:(t + 1) * width]
        diag_ref[...] = value

    def columns():
        arrived(column.at[group(row_y)], near_recv)
        arrived(column.at[group(row_far)], late_recv)

    shared(1)
    send_sum(0)
    shared(0)
    keep_sum(0)
    for s in range(cols):
        column[r * cols + s] = slab[s, me]
        column[row_x * cols + s] = slab_x[s, 0, c]
    for i in range(1, count):
        send_sum(i)
        keep_sum(i)
        if i >= LAG:
            if i == LAG:
                columns()
            finish(i - LAG, *chunks[i - LAG], None)
    if count <= LAG:
        columns()
    for i in range(max(count - LAG, 0), count - 2):
        finish(i, *chunks[i], None)
    arrived(xsum, x_recv)
    finish(count, split, total, xsum)
    finish(count - 2, *chunks[count - 2], None)
    finish(count - 1, *chunks[count - 1], None)
    for place, sem in (
        (green_x, green_sent), (slab_x.at[0], panel_sent), (slab.at[pl.ds(0, cols - 1)], slab_sent),
        (slab_x.at[pl.ds(0, cols - 1)], share_sent), (column.at[pl.ds(0, cols)], near_sent),
        (column.at[pl.ds(0, cols)], late_sent), (own.at[pl.ds(0, cols - 1)], own_sent), (ysum, y_sent),
        (far_out, far_sent), (to_x, x_sent),
    ):
        arrived(place, sem)


def store(made, grown, out_ref, diag_ref, sems):
    copies = [pltpu.make_async_copy(made, out_ref, sems.at[0]), pltpu.make_async_copy(grown, diag_ref, sems.at[1])]
    for copy in copies:
        copy.start()
    for copy in copies:
        copy.wait()


def local(green_blocks, lower_panel, pattern, pivot_inverse):
    rows, cols = lax.axis_size("row"), lax.axis_size("col")
    share, supernodes, width = lower_panel.shape
    vmem = pl.BlockSpec(memory_space=pltpu.VMEM)
    hbm = pl.BlockSpec(memory_space=pltpu.HBM)
    bf16 = lambda *shape: pltpu.VMEM(shape, jnp.bfloat16)
    dma = lambda *shape: pltpu.SemaphoreType.DMA(shape)
    total = rows * share
    green = green_blocks.reshape(total, -1)
    depth = green.shape[1]
    chunks = plan(total)
    count, split = len(chunks), chunks[-1][1]
    buffers = [
        bf16(total, depth),
        bf16(split, depth),
        bf16(*lower_panel.shape),
        pltpu.VMEM((share * supernodes, width), jnp.float32),
        pltpu.VMEM((width, width), jnp.float32),
        bf16(cols, supernodes, share, width),
        bf16(cols, 2, cols, share, width),
        bf16(rows * cols, share, width),
        bf16(cols, total, width),
        bf16(cols, total, width),
        bf16(cols, total, width),
        bf16(cols, total, width),
        bf16(cols, total - split, width),
        bf16(cols, total - split, width),
        bf16(cols, total - split, width),
        bf16(cols, total - split, width),
    ]
    held = sum(math.prod(b.shape) * jnp.dtype(b.dtype).itemsize for b in buffers)
    middle = pl.pallas_call(
        functools.partial(exchange, rows, cols),
        out_shape=(
            pltpu.VMEM((cols * total, width), jnp.bfloat16),
            pltpu.VMEM((width, width), jnp.float32),
        ),
        in_specs=[hbm] * 4,
        out_specs=(vmem,) * 2,
        scratch_shapes=[pltpu.SMEM(pattern.shape[::-1], pattern.dtype)] + buffers + [
            dma(4), dma(count), dma(count + 1), dma(count + 1), dma(2), dma(2), dma(5), dma(10),
        ],
        compiler_params=pltpu.CompilerParams(
            collective_id=0, has_side_effects=True, vmem_limit_bytes=held + held // 4 + 4 * 1024 * 1024,
        ),
    )(*(pltpu.with_memory_space_constraint(a, pltpu.HBM) for a in (pattern.T, green, lower_panel, pivot_inverse.reshape(width, width))))
    out, diag = pl.pallas_call(
        store,
        out_shape=(
            jax.ShapeDtypeStruct((cols * total, width), jnp.bfloat16),
            jax.ShapeDtypeStruct((width, width), jnp.float32),
        ),
        in_specs=[vmem] * 2,
        out_specs=(hbm, hbm),
        scratch_shapes=[dma(2)],
        compiler_params=pltpu.CompilerParams(vmem_limit_bytes=16 * 1024 * 1024),
    )(*middle)
    return out.reshape(-1, 1, width), diag.reshape(1, width, width)


def solution(mesh):
    placed = (
        P("pole", "col", None, "row"),
        P(("row", "col"), "pole", None),
        P(),
        P(("row", "col"), "pole", None),
    )
    return jax.shard_map(
        local,
        mesh=mesh,
        in_specs=placed,
        out_specs=(P("pole", ("row", "col"), None), P(("row", "col"), "pole", None)),
        check_vma=False,
    )
```

```python
import functools
import math

import jax
import jax.numpy as jnp
from jax import lax
from jax.experimental import pallas as pl
from jax.experimental.pallas import tpu as pltpu
from jax.sharding import PartitionSpec as P

MESH = pl.DeviceIdType.MESH
PAIR = 2
LAG = 2
AHEAD = 1
STEPS = (10, 10, 7, 3)


def plan(total):
    unit = total // 48
    ends = [0]
    for step in STEPS:
        ends.append(ends[-1] + step * unit)
    return list(zip(ends[:-1], ends[1:]))


def exchange(
    rows, cols, pattern_hbm, green_hbm, panel_hbm, pivot_hbm,
    out_ref, diag_ref,
    pattern_ref, green, green_x, panel_ref, wide, pivot_ref, slab, slab_x, column,
    own, to_own, ysum, to_y, far_out, far_in, to_x, xsum,
    load, green_recv, y_recv, own_recv, panel_recv, share_recv, one_recv, sent,
):
    r, c = lax.axis_index("row"), lax.axis_index("col")
    me = r * cols + c
    share, supernodes, width = panel_ref.shape
    row_x, row_y, row_far = r + 1 - 2 * (r % 2), (r + 2) % 4, 3 - r
    total = rows * share
    chunks = plan(total)
    count = len(chunks)
    split = chunks[-1][1]
    tail = slice(split, total)
    slab_recv, near_recv, late_recv, far_recv, x_recv = (one_recv.at[i] for i in range(5))
    (
        green_sent, panel_sent, slab_sent, share_sent, near_sent, late_sent, own_sent, y_sent, far_sent, x_sent
    ) = (sent.at[i] for i in range(10))

    def start(src, dst, send, recv, row, col):
        pltpu.make_async_remote_copy(
            src_ref=src, dst_ref=dst, send_sem=send, recv_sem=recv,
            device_id={"row": row, "col": col}, device_id_type=MESH,
        ).start()

    def arrived(place, recv):
        pltpu.make_async_copy(place, place, recv).wait()

    others = [(c + step) % cols for step in range(1, cols)]
    barrier = pltpu.get_barrier_semaphore()
    for row in (row_x, row_y):
        for k in range(cols):
            pl.semaphore_signal(barrier, 1, device_id={"row": row, "col": k}, device_id_type=MESH)
    for k in others:
        pl.semaphore_signal(barrier, 1, device_id={"row": r, "col": k}, device_id_type=MESH)
    loads = [
        pltpu.make_async_copy(panel_hbm, panel_ref, load.at[0]),
        pltpu.make_async_copy(pattern_hbm, pattern_ref, load.at[3]),
        pltpu.make_async_copy(green_hbm, green, load.at[1]),
        pltpu.make_async_copy(pivot_hbm, pivot_ref, load.at[2]),
    ]
    for copy in loads:
        copy.start()

    loads[0].wait()
    loads[1].wait()
    wide[...] = panel_ref[...].astype(jnp.float32).reshape(share * supernodes, width)
    piece = math.gcd(share, width)
    for k in range(supernodes):
        value = wide[pl.ds(k, share, stride=supernodes), :]
        parts = []
        for q in range(share // piece):
            flag = pattern_ref[k, (me * share + q * piece) // width].astype(jnp.float32)
            parts.append(value[q * piece:(q + 1) * piece] * flag)
        slab[c, k] = jnp.concatenate(parts, axis=0).astype(jnp.bfloat16)
    loads[2].wait()
    loads[3].wait()
    diag_ref[...] = pivot_ref[...]
    pl.semaphore_wait(barrier, 3 * cols - 1)

    def group(row):
        return pl.ds(row * cols, cols)

    def send_panel(g, row):
        start(slab.at[c, group(row)], slab_x.at[c, g], panel_sent, panel_recv.at[g], row_x, c)

    def send_green(i):
        low, high = chunks[i]
        span = pl.ds(low, high - low)
        start(green.at[span], green_x.at[span], green_sent, green_recv.at[i], row_x, c)

    send_panel(1, row_far)
    for k in others:
        start(slab.at[c], slab.at[c], slab_sent, slab_recv, r, k)
    for k in range(cols):
        start(slab.at[c, row_y * cols + k], column.at[me], near_sent, near_recv, row_y, k)
    for i in range(count):
        if i == AHEAD:
            send_panel(0, row_x)
        send_green(i)

    def pairs(body):
        if cols == PAIR:
            body(0)
        else:
            lax.fori_loop(0, cols // PAIR, lambda i, z: (body(i * PAIR), z)[1], 0)

    def stack(pick, k):
        return jnp.concatenate(
            [jnp.concatenate([pick(s, k + p) for s in range(cols)], axis=0) for p in range(PAIR)], axis=1
        )

    def product(buffer, at, lhs, rhs):
        def body(k):
            value = jnp.dot(lhs(), rhs(k), preferred_element_type=jnp.float32).astype(jnp.bfloat16)
            for p in range(PAIR):
                buffer[k + p, at] = value[:, p * width:(p + 1) * width]

        pairs(body)

    def alone(buffer, at, row):
        product(buffer, at, lambda: green[tail], lambda k: stack(lambda s, q: slab[s, row * cols + q], k))

    def joint(buffer, i, g, row):
        at = slice(*chunks[i])
        product(
            buffer, at,
            lambda: jnp.concatenate([green[at], green_x[at]], axis=1),
            lambda k: jnp.concatenate(
                [stack(lambda s, q: slab[s, row * cols + q], k), stack(lambda s, q: slab_x[s, g, q], k)], axis=0
            ),
        )

    rest = pl.ds(split, total - split)
    arrived(slab.at[pl.ds(0, cols - 1)], slab_recv)
    alone(far_out, slice(None), row_far)
    start(far_out, far_in, far_sent, far_recv, row_y, c)
    alone(to_y, tail, row_y)
    for k in range(cols):
        start(to_y.at[k, rest], ysum.at[c, rest], y_sent, y_recv.at[count], row_y, k)
    alone(to_own, tail, r)
    for k in others:
        start(to_own.at[k, rest], own.at[c, rest], own_sent, own_recv.at[count], r, k)
    own[c, tail] = to_own[c, tail]
    alone(to_x, slice(None), row_x)

    def pass_on(g):
        arrived(slab_x.at[c, g], panel_recv.at[g])
        for k in others:
            start(slab_x.at[c, g], slab_x.at[c, g], share_sent, share_recv.at[g], r, k)

    def shared(g):
        arrived(slab_x.at[pl.ds(0, cols - 1), g], share_recv.at[g])

    pass_on(1)
    for k in range(cols):
        start(slab_x.at[c, 1, k], column.at[row_x * cols + c], late_sent, late_recv, row_y, k)
    def send_sum(i):
        low, high = chunks[i]
        span = pl.ds(low, high - low)
        arrived(green_x.at[span], green_recv.at[i])
        joint(to_y, i, 1, row_y)
        for k in range(cols):
            start(to_y.at[k, span], ysum.at[c, span], y_sent, y_recv.at[i], row_y, k)

    def keep_sum(i):
        low, high = chunks[i]
        span = pl.ds(low, high - low)
        joint(to_own, i, 0, r)
        for k in others:
            start(to_own.at[k, span], own.at[c, span], own_sent, own_recv.at[i], r, k)
        own[c, low:high] = to_own[c, low:high]

    def finish(i, low, high, late):
        span = pl.ds(low, high - low)
        arrived(own.at[pl.ds(0, cols - 1), span], own_recv.at[i])
        arrived(ysum.at[:, span], y_recv.at[i])
        lhs, rhs = [], []
        for k in range(cols):
            terms = [own[k, low:high], ysum[k, low:high]] + ([late[k]] if late is not None else [])
            rhs.append(jnp.concatenate(terms, axis=1))
            value = sum(term.astype(jnp.float32) for term in terms)
            cuts = sorted({low, high} | set(range(-(-low // piece) * piece, high, piece)))
            for first, end in zip(cuts[:-1], cuts[1:]):
                begin = (first // share * cols + k) * share + first % share
                flag = pattern_ref[me, begin // width].astype(jnp.float32)
                out_ref[begin:begin + end - first] = (-(value[first - low:end - low] * flag)).astype(jnp.bfloat16)
            cuts = sorted({low, high} | set(range(-(-low // share) * share, high, share)))
            for first, end in zip(cuts[:-1], cuts[1:]):
                a = first % share
                lhs.append(column[first // share * cols + k, a:a + end - first])
        grown = lax.dot_general(
            jnp.concatenate(lhs, axis=0), jnp.concatenate(rhs, axis=0),
            (((0,), (0,)), ((), ())), preferred_element_type=jnp.float32,
        )
        value = diag_ref[...]
        for t in range(grown.shape[1] // width):
            value = value + grown[:, t * width:(t + 1) * width]
        diag_ref[...] = value

    def columns():
        arrived(column.at[group(row_y)], near_recv)
        arrived(column.at[group(row_far)], late_recv)

    shared(1)
    for i in range(AHEAD):
        send_sum(i)
    arrived(far_in, far_recv)
    to_x[...] = (to_x[...].astype(jnp.float32) + far_in[...].astype(jnp.float32)).astype(jnp.bfloat16)
    for k in range(cols):
        start(to_x.at[k], xsum.at[c], x_sent, x_recv, row_x, k)
    pass_on(0)
    for i in range(AHEAD, count):
        send_sum(i)
        if i == AHEAD:
            shared(0)
            for s in range(cols):
                column[r * cols + s] = slab[s, me]
                column[row_x * cols + s] = slab_x[s, 0, c]
            for h in range(AHEAD):
                keep_sum(h)
        keep_sum(i)
        if i >= LAG:
            if i == LAG:
                columns()
            finish(i - LAG, *chunks[i - LAG], None)
    if count <= LAG:
        columns()
    for i in range(max(count - LAG, 0), count - 2):
        finish(i, *chunks[i], None)
    arrived(xsum, x_recv)
    finish(count, split, total, xsum)
    finish(count - 2, *chunks[count - 2], None)
    finish(count - 1, *chunks[count - 1], None)
    for place, sem in (
        (green_x, green_sent), (slab_x.at[0], panel_sent), (slab.at[pl.ds(0, cols - 1)], slab_sent),
        (slab_x.at[pl.ds(0, cols - 1)], share_sent), (column.at[pl.ds(0, cols)], near_sent),
        (column.at[pl.ds(0, cols)], late_sent), (own.at[pl.ds(0, cols - 1)], own_sent), (ysum, y_sent),
        (far_out, far_sent), (to_x, x_sent),
    ):
        arrived(place, sem)


def store(made, grown, out_ref, diag_ref, sems):
    copies = [pltpu.make_async_copy(made, out_ref, sems.at[0]), pltpu.make_async_copy(grown, diag_ref, sems.at[1])]
    for copy in copies:
        copy.start()
    for copy in copies:
        copy.wait()


def local(green_blocks, lower_panel, pattern, pivot_inverse):
    rows, cols = lax.axis_size("row"), lax.axis_size("col")
    share, supernodes, width = lower_panel.shape
    vmem = pl.BlockSpec(memory_space=pltpu.VMEM)
    hbm = pl.BlockSpec(memory_space=pltpu.HBM)
    bf16 = lambda *shape: pltpu.VMEM(shape, jnp.bfloat16)
    dma = lambda *shape: pltpu.SemaphoreType.DMA(shape)
    total = rows * share
    green = green_blocks.reshape(total, -1)
    depth = green.shape[1]
    chunks = plan(total)
    count, split = len(chunks), chunks[-1][1]
    buffers = [
        bf16(total, depth),
        bf16(split, depth),
        bf16(*lower_panel.shape),
        pltpu.VMEM((share * supernodes, width), jnp.float32),
        pltpu.VMEM((width, width), jnp.float32),
        bf16(cols, supernodes, share, width),
        bf16(cols, 2, cols, share, width),
        bf16(rows * cols, share, width),
        bf16(cols, total, width),
        bf16(cols, total, width),
        bf16(cols, total, width),
        bf16(cols, total, width),
        bf16(cols, total - split, width),
        bf16(cols, total - split, width),
        bf16(cols, total - split, width),
        bf16(cols, total - split, width),
    ]
    held = sum(math.prod(b.shape) * jnp.dtype(b.dtype).itemsize for b in buffers)
    middle = pl.pallas_call(
        functools.partial(exchange, rows, cols),
        out_shape=(
            pltpu.VMEM((cols * total, width), jnp.bfloat16),
            pltpu.VMEM((width, width), jnp.float32),
        ),
        in_specs=[hbm] * 4,
        out_specs=(vmem,) * 2,
        scratch_shapes=[pltpu.SMEM(pattern.shape[::-1], pattern.dtype)] + buffers + [
            dma(4), dma(count), dma(count + 1), dma(count + 1), dma(2), dma(2), dma(5), dma(10),
        ],
        compiler_params=pltpu.CompilerParams(
            collective_id=0, has_side_effects=True, vmem_limit_bytes=held + held // 4 + 4 * 1024 * 1024,
        ),
    )(*(pltpu.with_memory_space_constraint(a, pltpu.HBM) for a in (pattern.T, green, lower_panel, pivot_inverse.reshape(width, width))))
    out, diag = pl.pallas_call(
        store,
        out_shape=(
            jax.ShapeDtypeStruct((cols * total, width), jnp.bfloat16),
            jax.ShapeDtypeStruct((width, width), jnp.float32),
        ),
        in_specs=[vmem] * 2,
        out_specs=(hbm, hbm),
        scratch_shapes=[dma(2)],
        compiler_params=pltpu.CompilerParams(vmem_limit_bytes=16 * 1024 * 1024),
    )(*middle)
    return out.reshape(-1, 1, width), diag.reshape(1, width, width)


def solution(mesh):
    placed = (
        P("pole", "col", None, "row"),
        P(("row", "col"), "pole", None),
        P(),
        P(("row", "col"), "pole", None),
    )
    return jax.shard_map(
        local,
        mesh=mesh,
        in_specs=placed,
        out_specs=(P("pole", ("row", "col"), None), P(("row", "col"), "pole", None)),
        check_vma=False,
    )
```
